32 devices in a mesh: dp: 4 (over z), tp: 8 (over y, x, core).
Axes of the slice: x: 2, y: 2, z: 4, core: 2. Of those that a mesh axis runs over, the one named last changes fastest.
Arguments:
- head_fsdp: bfloat16 [4096, 128256], P(('dp', 'tp')), may hold values from -0.5 to 0.5
- hidden: bfloat16 [1024, 4096], P(('dp', 'tp')), may hold values from -48 to 48
- targets: int32 [1024], P(('dp', 'tp')), may hold values from 0 to 128255
Outputs:
- head_tp: bfloat16 [4096, 128256], P('dp', 'tp')
- log_norm: float32 [1024], P(('dp', 'tp'))
- target_logprob: float32 [1024], P(('dp', 'tp'))
The draws below stay inside these ranges and needn't reach their ends.
All inputs are finite; a program needn't handle non-finite values.
Results may differ from the reference program's by a relative error of at most 0.0004.
Values may be sent and summed in bfloat16 or wider, within the bound.
A program may use at most 256 MiB of HBM per device.

```python
import jax
import jax.numpy as jnp
from jax import lax

D = 4096
V = 128256
SEQS = 256
BATCH = 1024
N_DP = 4


def draw_head_fsdp(key, part):
    values = jax.random.normal(jax.random.fold_in(key, 1), (D, V), jnp.float32)
    values = jnp.clip(values, -6.0, 6.0) * D ** (-0.5)
    return jnp.clip(values, -0.5, 0.5).astype(jnp.bfloat16)


def draw_hidden(key, part):
    noise = jnp.clip(jax.random.normal(jax.random.fold_in(key, 2), (BATCH, D), jnp.float32), -6.0, 6.0)
    values = 3.5 * noise
    return jnp.clip(values, -48.0, 48.0).astype(jnp.bfloat16)


def with_ends(drawn, own_key, smallest, largest):
    longest = drawn.shape.index(max(drawn.shape))
    spots = []
    for shift in (0, 1):
        where = [jax.random.randint(jax.random.fold_in(own_key, axis), (), 0, length) for axis, length in enumerate(drawn.shape)]
        where[longest] = (where[longest] + shift) % drawn.shape[longest]
        spots.append(tuple(where))
    return drawn.at[spots[0]].set(smallest).at[spots[1]].set(largest)


def setup_inputs(seed: int = 0) -> dict:
    arg_keys = jax.random.split(jax.random.key(seed), 4)
    return {
        "head_fsdp": draw_head_fsdp(jax.random.fold_in(arg_keys[3], 71), 0),
        "hidden": draw_hidden(jax.random.fold_in(arg_keys[3], 71), 0),
        "targets": with_ends(jax.random.randint(arg_keys[2], (BATCH,), 0, V), jax.random.fold_in(arg_keys[2], 1), 0, V - 1).astype(jnp.int32),
    }


def reference(head_fsdp, hidden, targets):
    hidden_blocks = hidden.reshape(N_DP, SEQS, D)
    target_blocks = targets.reshape(N_DP, SEQS)

    def score(pair):
        rows_hidden, rows_target = pair
        logits = jnp.dot(rows_hidden, head_fsdp, preferred_element_type=jnp.float32)
        top_logit = jnp.max(logits, axis=1)
        log_norm = top_logit + jnp.log(jnp.sum(jnp.exp(logits - top_logit[:, None]), axis=1))
        picked = jnp.take_along_axis(logits, rows_target[:, None].astype(jnp.int32), axis=1)[:, 0]
        return log_norm, picked - log_norm

    log_norm, logprob = lax.map(score, (hidden_blocks, target_blocks))
    return head_fsdp, log_norm.reshape(BATCH), logprob.reshape(BATCH)
```

```python
import functools

import jax
import jax.numpy as jnp
from jax import lax
from jax.experimental import pallas as pl
from jax.experimental.pallas import tpu as pltpu
from jax.sharding import PartitionSpec as P

MESH = pl.DeviceIdType.MESH
CHUNKS = 8
AHEAD = 3
TILE = 512
LOWEST = -3.0e38


def round_up(n, m):
    return -(-n // m) * m


def plan(columns, n_dp, chunks):
    share = round_up(-(-columns // (n_dp * chunks)), 8)
    steps, start, place = [], 0, 0
    while start < columns:
        rows = min(share * n_dp, columns - start)
        part = round_up(-(-rows // n_dp), 8)
        steps.append((start, rows, part, place))
        start += rows
        place += part
    return steps, place


def part_start(peer, rows, part):
    return pl.multiple_of(jnp.minimum(peer * part, rows - part), 8)


def exchange(n_dp, n_tp, steps, head, hid, tgt, mid, full, all_hid, all_tgt, own_a, own_b, own_h, own_t,
             a_send, a_recv, b_send, b_recv, h_send, h_recv, g_send, g_recv, local):
    z, t = lax.axis_index("dp"), lax.axis_index("tp")
    depth = hid.shape[0]
    width = head.shape[1]
    columns = mid.shape[0]
    zs = [lax.rem(z + j, n_dp) for j in range(n_dp)]
    ts = [lax.rem(t + j, n_tp) for j in range(n_tp)]
    barrier = pltpu.get_barrier_semaphore()
    for peer in zs[1:]:
        pl.semaphore_signal(barrier, inc=1, device_id=(peer, t), device_id_type=MESH)
    for peer in ts[1:]:
        pl.semaphore_signal(barrier, inc=1, device_id=(z, peer), device_id_type=MESH)
    n = len(steps)
    lane = pl.ds(pl.multiple_of(t * width, width), width)
    block = pl.ds(pl.multiple_of(z * mid.shape[1], mid.shape[1]), mid.shape[1])

    loads = []
    for c, (start, rows, part, place) in enumerate(steps):
        copy = pltpu.make_async_copy(
            head.at[pl.ds(pl.multiple_of(t * columns + start, 8), rows)], own_a.at[pl.ds(start, rows)], local.at[0, c])
        copy.start()
        loads.append(copy)
    in_h = pltpu.make_async_copy(hid, own_h, local.at[4, 0])
    in_t = pltpu.make_async_copy(tgt, own_t, local.at[4, 1])
    in_h.start()
    in_t.start()
    pl.semaphore_wait(barrier, n_dp + n_tp - 2)

    def send_a(c):
        start, rows, part, place = steps[c]
        copies = []
        for j in range(1, n_tp):
            copy = pltpu.make_async_remote_copy(
                src_ref=head.at[pl.ds(pl.multiple_of(ts[j] * columns + start, 8), rows)],
                dst_ref=mid.at[pl.ds(start, rows), lane],
                send_sem=a_send.at[c, j - 1], recv_sem=a_recv.at[c, j - 1],
                device_id=(z, ts[j]), device_id_type=MESH)
            copy.start()
            copies.append(copy)
        return copies

    sent_a = [send_a(c) for c in range(min(AHEAD, n))]

    small = []
    for j in range(1, n_dp):
        for k, (src, dst) in enumerate(((hid, all_hid), (tgt, all_tgt))):
            copy = pltpu.make_async_remote_copy(
                src_ref=src, dst_ref=dst.at[t, z], send_sem=h_send.at[k, j - 1], recv_sem=h_recv.at[k, j - 1],
                device_id=(zs[j], t), device_id_type=MESH)
            copy.start()
            small.append(copy)
    in_h.wait()
    in_t.wait()
    out_h = pltpu.make_async_copy(own_h, all_hid.at[t, z], local.at[4, 2])
    out_t = pltpu.make_async_copy(own_t, all_tgt.at[t, z], local.at[4, 3])
    out_h.start()
    out_t.start()
    stores = []
    for c, (start, rows, part, place) in enumerate(steps):
        loads[c].wait()
        copy = pltpu.make_async_copy(own_a.at[pl.ds(start, rows)], mid.at[pl.ds(start, rows), lane], local.at[1, c])
        copy.start()
        stores.append(copy)

    sent_b, ins_b, outs_b, spread = [], [], [], []

    def keep_b(c):
        start, rows, part, place = steps[c]
        ins_b[c].wait()
        copy = pltpu.make_async_copy(own_b.at[pl.ds(place, part)], full.at[pl.ds(place, part), block], local.at[3, c])
        copy.start()
        outs_b.append(copy)

    for c, (start, rows, part, place) in enumerate(steps):
        stores[c].wait()
        for copy in sent_a[c]:
            copy.wait_recv()
        for j in range(1, n_dp):
            copy = pltpu.make_async_remote_copy(
                src_ref=mid.at[pl.ds(start + part_start(zs[j], rows, part), part)],
                dst_ref=full.at[pl.ds(place, part), block],
                send_sem=b_send.at[c, j - 1], recv_sem=b_recv.at[c, j - 1],
                device_id=(zs[j], t), device_id_type=MESH)
            copy.start()
            sent_b.append(copy)
        copy = pltpu.make_async_copy(
            mid.at[pl.ds(start + part_start(z, rows, part), part)], own_b.at[pl.ds(place, part)], local.at[2, c])
        copy.start()
        ins_b.append(copy)
        if c + AHEAD < n:
            sent_a.append(send_a(c + AHEAD))
        if c >= 1:
            keep_b(c - 1)
        if c == min(1, n - 1):
            out_h.wait()
            out_t.wait()
            for copy in small:
                copy.wait_recv()
            for j in range(1, n_tp):
                for k, ref in enumerate((all_hid, all_tgt)):
                    copy = pltpu.make_async_remote_copy(
                        src_ref=ref.at[t], dst_ref=ref.at[t], send_sem=g_send.at[k, j - 1], recv_sem=g_recv.at[k, j - 1],
                        device_id=(z, ts[j]), device_id_type=MESH)
                    copy.start()
                    spread.append(copy)
    keep_b(n - 1)
    for copy in sent_b + spread:
        copy.wait()
    for copies in sent_a:
        for copy in copies:
            copy.wait_send()
    for copy in small:
        copy.wait_send()
    for copy in outs_b:
        copy.wait()


def score(ids_ref, tgt_ref, hid_ref, w_ref, mid_ref, head_ref, out_ref, peak, mass, pick):
    step = pl.program_id(0)

    @pl.when(step == 0)
    def _():
        peak[...] = jnp.full_like(peak, LOWEST)
        mass[...] = jnp.zeros_like(mass)
        pick[...] = jnp.zeros_like(pick)

    head_ref[...] = mid_ref[...]
    logits = lax.dot_general(w_ref[...], hid_ref[...], (((1,), (1,)), ((), ())), preferred_element_type=jnp.float32)
    ids = ids_ref[...]
    pick[...] += jnp.sum(jnp.where(ids == tgt_ref[...], logits, 0.0), axis=0, keepdims=True)
    logits = jnp.where(ids >= 0, logits, LOWEST)
    old = peak[...]
    new = jnp.maximum(old, jnp.max(logits, axis=0, keepdims=True))
    mass[...] = mass[...] * jnp.exp(old - new) + jnp.sum(jnp.exp(logits - new), axis=0, keepdims=True)
    peak[...] = new

    @pl.when(step == pl.num_programs(0) - 1)
    def _():
        out_ref[0:1, :] = peak[...]
        out_ref[1:2, :] = mass[...]
        out_ref[2:3, :] = pick[...]
        out_ref[3:8, :] = jnp.zeros((5, out_ref.shape[1]), jnp.float32)


def shards(n_dp, n_tp, head_fsdp, hidden, targets):
    width, vocab = head_fsdp.shape
    if width % 128 or (vocab // n_tp) % 8 or hidden.shape[0] % 8:
        return plain_shards(head_fsdp, hidden, targets)
    own, model = hidden.shape
    columns = vocab // n_tp
    batch = own * n_dp * n_tp
    steps, part = plan(columns, n_dp, CHUNKS)
    n = len(steps)
    lanes = round_up(own, 128)
    tgt = jnp.broadcast_to(jnp.pad(targets, (0, lanes - own))[None, :], (8, lanes))
    anyspace = pl.BlockSpec(memory_space=pl.ANY)
    bf16 = jnp.bfloat16
    dma = pltpu.SemaphoreType.DMA
    mid, full, all_hid, all_tgt = pl.pallas_call(
        functools.partial(exchange, n_dp, n_tp, steps),
        out_shape=[
            jax.ShapeDtypeStruct((columns, n_tp * width), bf16),
            jax.ShapeDtypeStruct((part, model), bf16),
            jax.ShapeDtypeStruct((n_tp, n_dp, own, model), bf16),
            jax.ShapeDtypeStruct((n_tp, n_dp, 8, lanes), jnp.int32),
        ],
        in_specs=[anyspace] * 3,
        out_specs=[anyspace] * 4,
        scratch_shapes=[
            pltpu.VMEM((columns, width), bf16),
            pltpu.VMEM((part, n_tp * width), bf16),
            pltpu.VMEM((own, model), bf16),
            pltpu.VMEM((8, lanes), jnp.int32),
            dma((n, n_tp - 1)), dma((n, n_tp - 1)),
            dma((n, n_dp - 1)), dma((n, n_dp - 1)),
            dma((2, n_dp - 1)), dma((2, n_dp - 1)),
            dma((2, n_tp - 1)), dma((2, n_tp - 1)),
            dma((5, max(n, 4))),
        ],
        compiler_params=pltpu.CompilerParams(
            collective_id=0, has_side_effects=True, vmem_limit_bytes=60 * 2**20),
        name="exchange",
    )(head_fsdp.T, hidden, tgt)

    z, t = lax.axis_index("dp"), lax.axis_index("tp")
    grid = -(-part // TILE)
    ids = []
    for start, rows, share, _ in steps:
        first = jnp.minimum(z * share, rows - share)
        row = first + jnp.arange(share, dtype=jnp.int32)
        ids.append(jnp.where(row >= z * share, t * columns + start + row, -1))
    ids = jnp.pad(jnp.concatenate(ids), (0, grid * TILE - part), constant_values=-1)[:, None]
    all_targets = all_tgt[:, :, 0, :own].reshape(1, batch)
    keep = round_up(-(-columns // grid), 16)
    head_t, local = pl.pallas_call(
        score,
        grid=(grid,),
        out_shape=[
            jax.ShapeDtypeStruct((columns, n_tp * width), bf16),
            jax.ShapeDtypeStruct((8, batch), jnp.float32),
        ],
        in_specs=[
            pl.BlockSpec((TILE, 1), lambda i: (i, 0)),
            pl.BlockSpec((1, batch), lambda i: (0, 0)),
            pl.BlockSpec((batch, model), lambda i: (0, 0), pipeline_mode=pl.Buffered(1)),
            pl.BlockSpec((TILE, model), lambda i: (i, 0)),
            pl.BlockSpec((keep, n_tp * width), lambda i: (i, 0)),
        ],
        out_specs=[
            pl.BlockSpec((keep, n_tp * width), lambda i: (i, 0)),
            pl.BlockSpec((8, batch), lambda i: (0, 0)),
        ],
        scratch_shapes=[pltpu.VMEM((1, batch), jnp.float32)] * 3,
        compiler_params=pltpu.CompilerParams(vmem_limit_bytes=60 * 2**20),
        name="score",
    )(ids, all_targets, all_hid.reshape(batch, model), full, mid)

    pieces = local[:3].reshape(3, n_tp, n_dp, own).transpose(2, 1, 0, 3).reshape(n_dp * n_tp, 3 * own)
    pieces = lax.all_to_all(pieces, ("dp", "tp"), split_axis=0, concat_axis=0, tiled=True)
    peaks, masses, picks = (pieces[:, i * own:(i + 1) * own] for i in range(3))
    top = jnp.max(peaks, axis=0)
    log_norm = top + jnp.log(jnp.sum(masses * jnp.exp(peaks - top[None, :]), axis=0))
    return head_t.T, log_norm, jnp.sum(picks, axis=0) - log_norm


def plain_shards(head_fsdp, hidden, targets):
    head_tp = lax.all_to_all(head_fsdp, "tp", split_axis=1, concat_axis=0, tiled=True)
    head_full = lax.all_to_all(head_fsdp, ("dp", "tp"), split_axis=1, concat_axis=0, tiled=True)
    vocab_start = (
        lax.axis_index("dp") * lax.axis_size("tp") + lax.axis_index("tp")
    ) * head_full.shape[1]
    all_hidden, all_targets = (
        lax.all_gather(hidden, ("dp", "tp"), axis=0, tiled=True),
        lax.all_gather(targets, ("dp", "tp"), axis=0, tiled=True),
    )
    logits = jnp.dot(all_hidden, head_full, preferred_element_type=jnp.float32)
    local_peak = jnp.max(logits, axis=1)
    offset = all_targets - vocab_start
    columns = lax.broadcasted_iota(jnp.int32, logits.shape, 1)
    picked = jnp.sum(jnp.where(columns == offset[:, None], logits, 0.0), axis=1)
    top_logit = lax.pmax(local_peak, ("dp", "tp"))
    local_mass = jnp.sum(jnp.exp(logits - top_logit[:, None]), axis=1)
    total_mass, target_logit = lax.psum((local_mass, picked), ("dp", "tp"))
    log_norm = top_logit + jnp.log(total_mass)
    logprob = target_logit - log_norm
    own_rows = hidden.shape[0]
    row_start = (lax.axis_index("dp") * lax.axis_size("tp") + lax.axis_index("tp")) * own_rows
    own_norm = lax.dynamic_slice_in_dim(log_norm, row_start, own_rows, 0)
    own_logprob = lax.dynamic_slice_in_dim(logprob, row_start, own_rows, 0)
    return (head_tp, own_norm, own_logprob)


def solution(mesh):
    in_specs = (P(("dp", "tp"), None), P(("dp", "tp"), None), P(("dp", "tp")))
    out_specs = (P("dp", "tp"), P(("dp", "tp")), P(("dp", "tp")))
    body = functools.partial(shards, mesh.shape["dp"], mesh.shape["tp"])
    return jax.shard_map(body, mesh=mesh, in_specs=in_specs, out_specs=out_specs, check_vma=False)
```

```python
import functools

import jax
import jax.numpy as jnp
from jax import lax
from jax.experimental import pallas as pl
from jax.experimental.pallas import tpu as pltpu
from jax.sharding import PartitionSpec as P

MESH = pl.DeviceIdType.MESH
CHUNKS = 8
AHEAD = 3
TILE = 512
LOWEST = -3.0e38


def round_up(n, m):
    return -(-n // m) * m


def plan(columns, n_dp, chunks):
    full_share = round_up(-(-columns // (n_dp * chunks)), 8)
    share = round_up(-(-full_share // 8), 8)
    steps, start, place = [], 0, 0
    while start < columns:
        rows = min(share * n_dp, columns - start)
        part = round_up(-(-rows // n_dp), 8)
        steps.append((start, rows, part, place))
        start += rows
        place += part
        share = min(2 * share, full_share)
    return steps, place


def part_start(peer, rows, part):
    return pl.multiple_of(jnp.minimum(peer * part, rows - part), 8)


def spans(steps):
    out, place = [], 0
    for _, rows, _, _ in steps:
        length = round_up(rows + 120, 128)
        out.append((place, length))
        place += length
    return out, place


def exchange(n_dp, n_tp, steps, head, hid, tgt, mid, full, all_hid, all_tgt, stage, cols_in, rows_out, t_sem, own_a, own_b, own_h, own_t,
             a_send, a_recv, b_send, b_recv, h_send, h_recv, g_send, g_recv, local):
    z, t = lax.axis_index("dp"), lax.axis_index("tp")
    depth = hid.shape[0]
    width, vocab = head.shape
    columns = mid.shape[0]
    zs = [lax.rem(z + j, n_dp) for j in range(n_dp)]
    ts = [lax.rem(t + j, n_tp) for j in range(n_tp)]
    barrier = pltpu.get_barrier_semaphore()
    for peer in zs[1:]:
        pl.semaphore_signal(barrier, inc=1, device_id=(peer, t), device_id_type=MESH)
    for peer in ts[1:]:
        pl.semaphore_signal(barrier, inc=1, device_id=(z, peer), device_id_type=MESH)
    n = len(steps)
    lane = pl.ds(pl.multiple_of(t * width, width), width)
    block = pl.ds(pl.multiple_of(z * mid.shape[1], mid.shape[1]), mid.shape[1])

    places, _ = spans(steps)

    def source(c, j):
        start, rows, _, _ = steps[c]
        place, length = places[c]
        first = ts[j] * columns + start
        base = jnp.minimum(first // 128 * 128, vocab - length)
        return base, stage.at[j, pl.ds(pl.multiple_of(place + first - base, 8), rows)]

    def turn(c):
        place, length = places[c]
        copies = []
        for j in range(n_tp):
            base, _ = source(c, j)
            copy = pltpu.make_async_copy(
                head.at[:, pl.ds(pl.multiple_of(base, 128), length)], cols_in.at[j, :, pl.ds(0, length)], t_sem.at[0, j])
            copy.start()
            copies.append(copy)
        outs = []
        for j in range(n_tp):
            copies[j].wait()

            def tile(k, carry, j=j):
                at = pl.ds(pl.multiple_of(k * 128, 128), 128)
                rows_out[j, at, :] = cols_in[j, :, at].T
                return carry

            lax.fori_loop(0, length // 128, tile, 0)
            copy = pltpu.make_async_copy(
                rows_out.at[j, pl.ds(0, length)], stage.at[j, pl.ds(place, length)], t_sem.at[1, j])
            copy.start()
            outs.append(copy)
        for copy in outs:
            copy.wait()

    in_h = pltpu.make_async_copy(hid, own_h, local.at[4, 0])
    in_t = pltpu.make_async_copy(tgt, own_t, local.at[4, 1])
    in_h.start()
    in_t.start()
    pl.semaphore_wait(barrier, n_dp + n_tp - 2)

    loads = []

    def send_a(c):
        start, rows, part, place = steps[c]
        turn(c)
        copies = []
        for j in range(1, n_tp):
            copy = pltpu.make_async_remote_copy(
                src_ref=source(c, j)[1],
                dst_ref=mid.at[pl.ds(start, rows), lane],
                send_sem=a_send.at[c, j - 1], recv_sem=a_recv.at[c, j - 1],
                device_id=(z, ts[j]), device_id_type=MESH)
            copy.start()
            copies.append(copy)
        copy = pltpu.make_async_copy(source(c, 0)[1], own_a.at[pl.ds(start, rows)], local.at[0, c])
        copy.start()
        loads.append(copy)
        return copies

    sent_a = [send_a(c) for c in range(min(AHEAD, n))]

    small = []
    for j in range(1, n_dp):
        for k, (src, dst) in enumerate(((hid, all_hid), (tgt, all_tgt))):
            copy = pltpu.make_async_remote_copy(
                src_ref=src, dst_ref=dst.at[t, z], send_sem=h_send.at[k, j - 1], recv_sem=h_recv.at[k, j - 1],
                device_id=(zs[j], t), device_id_type=MESH)
            copy.start()
            small.append(copy)
    in_h.wait()
    in_t.wait()
    out_h = pltpu.make_async_copy(own_h, all_hid.at[t, z], local.at[4, 2])
    out_t = pltpu.make_async_copy(own_t, all_tgt.at[t, z], local.at[4, 3])
    out_h.start()
    out_t.start()
    sent_b, ins_b, outs_b, spread = [], [], [], []

    def keep_b(c):
        start, rows, part, place = steps[c]
        ins_b[c].wait()
        copy = pltpu.make_async_copy(own_b.at[pl.ds(place, part)], full.at[pl.ds(place, part), block], local.at[3, c])
        copy.start()
        outs_b.append(copy)

    for c, (start, rows, part, place) in enumerate(steps):
        loads[c].wait()
        store = pltpu.make_async_copy(own_a.at[pl.ds(start, rows)], mid.at[pl.ds(start, rows), lane], local.at[1, c])
        store.start()
        store.wait()
        for copy in sent_a[c]:
            copy.wait_recv()
        for j in range(1, n_dp):
            copy = pltpu.make_async_remote_copy(
                src_ref=mid.at[pl.ds(start + part_start(zs[j], rows, part), part)],
                dst_ref=full.at[pl.ds(place, part), block],
                send_sem=b_send.at[c, j - 1], recv_sem=b_recv.at[c, j - 1],
                device_id=(zs[j], t), device_id_type=MESH)
            copy.start()
            sent_b.append(copy)
        copy = pltpu.make_async_copy(
            mid.at[pl.ds(start + part_start(z, rows, part), part)], own_b.at[pl.ds(place, part)], local.at[2, c])
        copy.start()
        ins_b.append(copy)
        if c + AHEAD < n:
            sent_a.append(send_a(c + AHEAD))
        if c >= 1:
            keep_b(c - 1)
        if c == min(1, n - 1):
            out_h.wait()
            out_t.wait()
            for copy in small:
                copy.wait_recv()
            for j in range(1, n_tp):
                for k, ref in enumerate((all_hid, all_tgt)):
                    copy = pltpu.make_async_remote_copy(
                        src_ref=ref.at[t], dst_ref=ref.at[t], send_sem=g_send.at[k, j - 1], recv_sem=g_recv.at[k, j - 1],
                        device_id=(z, ts[j]), device_id_type=MESH)
                    copy.start()
                    spread.append(copy)
    keep_b(n - 1)
    for copy in sent_b + spread:
        copy.wait()
    for copies in sent_a:
        for copy in copies:
            copy.wait_send()
    for copy in small:
        copy.wait_send()
    for copy in outs_b:
        copy.wait()


def score(ids_ref, tgt_ref, hid_ref, w_ref, mid_ref, head_ref, out_ref, peak, mass, pick):
    step = pl.program_id(0)

    @pl.when(step == 0)
    def _():
        peak[...] = jnp.full_like(peak, LOWEST)
        mass[...] = jnp.zeros_like(mass)
        pick[...] = jnp.zeros_like(pick)

    head_ref[...] = mid_ref[...]
    logits = lax.dot_general(w_ref[...], hid_ref[...], (((1,), (1,)), ((), ())), preferred_element_type=jnp.float32)
    ids = ids_ref[...]
    pick[...] += jnp.sum(jnp.where(ids == tgt_ref[...], logits, 0.0), axis=0, keepdims=True)
    logits = jnp.where(ids >= 0, logits, LOWEST)
    old = peak[...]
    new = jnp.maximum(old, jnp.max(logits, axis=0, keepdims=True))
    mass[...] = mass[...] * jnp.exp(old - new) + jnp.sum(jnp.exp(logits - new), axis=0, keepdims=True)
    peak[...] = new

    @pl.when(step == pl.num_programs(0) - 1)
    def _():
        out_ref[0:1, :] = peak[...]
        out_ref[1:2, :] = mass[...]
        out_ref[2:3, :] = pick[...]
        out_ref[3:8, :] = jnp.zeros((5, out_ref.shape[1]), jnp.float32)


def shards(n_dp, n_tp, head_fsdp, hidden, targets):
    width, vocab = head_fsdp.shape
    if width != 128 or vocab % 128 or (vocab // n_tp) % 8 or hidden.shape[0] % 8:
        return plain_shards(head_fsdp, hidden, targets)
    own, model = hidden.shape
    columns = vocab // n_tp
    batch = own * n_dp * n_tp
    steps, part = plan(columns, n_dp, CHUNKS)
    n = len(steps)
    lanes = round_up(own, 128)
    tgt = jnp.broadcast_to(jnp.pad(targets, (0, lanes - own))[None, :], (8, lanes))
    anyspace = pl.BlockSpec(memory_space=pl.ANY)
    bf16 = jnp.bfloat16
    dma = pltpu.SemaphoreType.DMA
    _, staged = spans(steps)
    widest = max(length for _, length in spans(steps)[0])
    mid, full, all_hid, all_tgt, _ = pl.pallas_call(
        functools.partial(exchange, n_dp, n_tp, steps),
        out_shape=[
            jax.ShapeDtypeStruct((columns, n_tp * width), bf16),
            jax.ShapeDtypeStruct((part, model), bf16),
            jax.ShapeDtypeStruct((n_tp, n_dp, own, model), bf16),
            jax.ShapeDtypeStruct((n_tp, n_dp, 8, lanes), jnp.int32),
            jax.ShapeDtypeStruct((n_tp, staged, width), bf16),
        ],
        in_specs=[anyspace] * 3,
        out_specs=[anyspace] * 5,
        scratch_shapes=[
            pltpu.VMEM((n_tp, width, widest), bf16),
            pltpu.VMEM((n_tp, widest, width), bf16),
            dma((2, n_tp)),
            pltpu.VMEM((columns, width), bf16),
            pltpu.VMEM((part, n_tp * width), bf16),
            pltpu.VMEM((own, model), bf16),
            pltpu.VMEM((8, lanes), jnp.int32),
            dma((n, n_tp - 1)), dma((n, n_tp - 1)),
            dma((n, n_dp - 1)), dma((n, n_dp - 1)),
            dma((2, n_dp - 1)), dma((2, n_dp - 1)),
            dma((2, n_tp - 1)), dma((2, n_tp - 1)),
            dma((5, max(n, 4))),
        ],
        compiler_params=pltpu.CompilerParams(
            collective_id=0, has_side_effects=True, vmem_limit_bytes=60 * 2**20),
        name="exchange",
    )(head_fsdp, hidden, tgt)

    z, t = lax.axis_index("dp"), lax.axis_index("tp")
    grid = -(-part // TILE)
    ids = []
    for start, rows, share, _ in steps:
        first = jnp.minimum(z * share, rows - share)
        row = first + jnp.arange(share, dtype=jnp.int32)
        ids.append(jnp.where(row >= z * share, t * columns + start + row, -1))
    ids = jnp.pad(jnp.concatenate(ids), (0, grid * TILE - part), constant_values=-1)[:, None]
    all_targets = all_tgt[:, :, 0, :own].reshape(1, batch)
    keep = round_up(-(-columns // grid), 16)
    head_t, local = pl.pallas_call(
        score,
        grid=(grid,),
        out_shape=[
            jax.ShapeDtypeStruct((columns, n_tp * width), bf16),
            jax.ShapeDtypeStruct((8, batch), jnp.float32),
        ],
        in_specs=[
            pl.BlockSpec((TILE, 1), lambda i: (i, 0)),
            pl.BlockSpec((1, batch), lambda i: (0, 0)),
            pl.BlockSpec((batch, model), lambda i: (0, 0), pipeline_mode=pl.Buffered(1)),
            pl.BlockSpec((TILE, model), lambda i: (i, 0)),
            pl.BlockSpec((keep, n_tp * width), lambda i: (i, 0)),
        ],
        out_specs=[
            pl.BlockSpec((keep, n_tp * width), lambda i: (i, 0)),
            pl.BlockSpec((8, batch), lambda i: (0, 0)),
        ],
        scratch_shapes=[pltpu.VMEM((1, batch), jnp.float32)] * 3,
        compiler_params=pltpu.CompilerParams(vmem_limit_bytes=60 * 2**20),
        name="score",
    )(ids, all_targets, all_hid.reshape(batch, model), full, mid)

    pieces = local[:3].reshape(3, n_tp, n_dp, own).transpose(2, 1, 0, 3).reshape(n_dp * n_tp, 3 * own)
    pieces = lax.all_to_all(pieces, ("dp", "tp"), split_axis=0, concat_axis=0, tiled=True)
    peaks, masses, picks = (pieces[:, i * own:(i + 1) * own] for i in range(3))
    top = jnp.max(peaks, axis=0)
    log_norm = top + jnp.log(jnp.sum(masses * jnp.exp(peaks - top[None, :]), axis=0))
    return head_t.T, log_norm, jnp.sum(picks, axis=0) - log_norm


def plain_shards(head_fsdp, hidden, targets):
    head_tp = lax.all_to_all(head_fsdp, "tp", split_axis=1, concat_axis=0, tiled=True)
    head_full = lax.all_to_all(head_fsdp, ("dp", "tp"), split_axis=1, concat_axis=0, tiled=True)
    vocab_start = (
        lax.axis_index("dp") * lax.axis_size("tp") + lax.axis_index("tp")
    ) * head_full.shape[1]
    all_hidden, all_targets = (
        lax.all_gather(hidden, ("dp", "tp"), axis=0, tiled=True),
        lax.all_gather(targets, ("dp", "tp"), axis=0, tiled=True),
    )
    logits = jnp.dot(all_hidden, head_full, preferred_element_type=jnp.float32)
    local_peak = jnp.max(logits, axis=1)
    offset = all_targets - vocab_start
    columns = lax.broadcasted_iota(jnp.int32, logits.shape, 1)
    picked = jnp.sum(jnp.where(columns == offset[:, None], logits, 0.0), axis=1)
    top_logit = lax.pmax(local_peak, ("dp", "tp"))
    local_mass = jnp.sum(jnp.exp(logits - top_logit[:, None]), axis=1)
    total_mass, target_logit = lax.psum((local_mass, picked), ("dp", "tp"))
    log_norm = top_logit + jnp.log(total_mass)
    logprob = target_logit - log_norm
    own_rows = hidden.shape[0]
    row_start = (lax.axis_index("dp") * lax.axis_size("tp") + lax.axis_index("tp")) * own_rows
    own_norm = lax.dynamic_slice_in_dim(log_norm, row_start, own_rows, 0)
    own_logprob = lax.dynamic_slice_in_dim(logprob, row_start, own_rows, 0)
    return (head_tp, own_norm, own_logprob)


def solution(mesh):
    in_specs = (P(("dp", "tp"), None), P(("dp", "tp"), None), P(("dp", "tp")))
    out_specs = (P("dp", "tp"), P(("dp", "tp")), P(("dp", "tp")))
    body = functools.partial(shards, mesh.shape["dp"], mesh.shape["tp"])
    return jax.shard_map(body, mesh=mesh, in_specs=in_specs, out_specs=out_specs, check_vma=False)
```
